32 devices in a mesh: groups: 2 (over y), sky: 4 (over z), shell: 2 (over x), sub: 2 (over core).
Axes of the slice: x: 2, y: 2, z: 4, core: 2. Of those that a mesh axis runs over, the one named last changes fastest.
Arguments:
- part_cycle: int32 [2, 2048, 256], P('shell', ('sky', 'sub')), may hold values from 0 to 1
- part_pixel: int32 [2, 2048, 256], P('shell', ('sky', 'sub')), may hold values from 0 to 127
- part_mass: float32 [2, 2048, 256], P('shell', ('sky', 'sub')), may hold values from 0.3 to 3
- tile_block: int32 [2, 2048, 1], P('shell', ('sky', 'sub')), may hold values from 0 to 7; in each aligned block of 256 rows (0 to 255, 256 to 511, ..., all dimensions but the last counted through in order) at most 128 rows name the same one
- tile_shell: int32 [2, 2048], P('shell', ('sky', 'sub')), may hold values from 0 to 1
- tile_pixel: int32 [2, 2048], P('shell', ('sky', 'sub')), may hold values from 0 to 63
- harmonic_basis: bfloat16 [128, 16, 4096], P('sky', 'sub'), may hold values from -1.5 to 1.5
- lens_weight: float32 [4, 4], replicated, may hold values from 0.2 to 1
Outputs:
- convergence: float32 [8, 128, 2, 4096], P(('groups', 'shell'), 'sky', None, 'sub'), parts along dimension 0
The draws below stay inside these ranges and needn't reach their ends.
There are 2 independent parts, one for each index of `groups`. The reference program is written for one: setup_inputs(seed, part) draws one part's arguments, and reference() takes and returns one part's arrays. A program takes and returns all parts, laid end to end along the dimension named above; an argument that names none is the same for every part. Nothing has to cross between parts.
Inputs may be any that keep to these rules, and one draw needn't show every extreme that they name: `tile_block`: among the rows of one device no cycle block is named by more than 128 tiles, and in some device one block is named by exactly 128.
All inputs are finite; a program needn't handle non-finite values.
Results may differ from the reference program's by a relative error of at most 0.0015.
Values may be sent and summed in bfloat16 or wider, within the bound.
No kernel may reach another device: no remote copies, remote signals or barrier semaphores. Data moves between devices by JAX's collectives and lax.ppermute only.
A program may use at most 192 MiB of HBM per device.

```python
import math
import jax
import jax.numpy as jnp
import numpy as np
from jax import lax

NP = 8192
M = 128
L = 4096
TP = 128
CYCLE_DEV = 2
SHELL_DEV = 2
TILES_DEV = 256
PART_TILE = 256
BLOCKS = 8
CYCLES = 16
NBLK = 64
CAP = 128
TILES_ROW = 2048
SHELLS = 4
SOURCES = 4
N_SHELL = 2


def touch_ends(drawn, rng, least, top_value):
    dims = drawn.shape
    index_at = [jax.random.randint(jax.random.fold_in(rng, axis), (), 0, dims[axis]) for axis in range(len(dims))]
    drawn = drawn.at[tuple(index_at)].set(least)
    longest = dims.index(max(dims))
    index_at[longest] = (index_at[longest] + 1) % dims[longest]
    return drawn.at[tuple(index_at)].set(top_value)


def level_of(own_key, dims, cuts, least, largest):
    def one(position, blocks):
        heights = jax.random.uniform(jax.random.fold_in(jax.random.fold_in(own_key, 6), position), (blocks,), jnp.float32, least / len(cuts), largest / len(cuts))
        return jnp.repeat(jnp.exp(heights), dims[position] // blocks).reshape((-1,) + (1,) * (len(dims) - position - 1))

    loudness = one(*cuts[0])
    for cut in cuts[1:]:
        loudness = loudness * one(*cut)
    return loudness


def deal_out(own_key, own, number, rows, number_of, top, most, skew):
    order = jax.random.permutation(own_key, number_of)
    heavy_load, common = shares(number_of, rows * top, most, skew, True), shares(number_of, rows * top, most, skew, False)
    places = jnp.arange(number_of)

    def named(tallies, turn):
        used = int((tallies > 0).sum())
        fixed = max(1, used // 4)
        passed = fixed + (places - fixed + turn * (used - fixed)) % max(1, number_of - fixed)
        return jnp.zeros((number_of,), jnp.int32).at[order[jnp.where(places < fixed, places, passed)]].set(jnp.asarray(tallies, jnp.int32))

    tallies = jnp.where(number % 4 == 0, named(heavy_load, number // 4), named(common, number - number // 4 - 1))
    mixed = jax.random.permutation(jax.random.fold_in(own, 3), number_of)
    source_of, sink = mixed[0:number_of // 2 * 2:2], mixed[1:number_of // 2 * 2:2]
    slack = jnp.minimum(tallies[source_of] - 1, most - tallies[sink]) // 2
    slack = jnp.where((source_of == order[0]) | (sink == order[0]) | (tallies[sink] == 0), 0, jnp.maximum(slack, 0))
    passed = jax.random.randint(jax.random.fold_in(own, 4), (number_of // 2,), 0, 1 << 20) % (slack + 1)
    tallies = tallies.at[source_of].add(-passed).at[sink].add(passed)
    members = jnp.searchsorted(jnp.cumsum(tallies), jnp.arange(rows * top), side="right").astype(jnp.int32)
    listing = members.reshape(top, rows).T
    listing = listing[jax.random.permutation(jax.random.fold_in(own, 1), rows)]
    turn = jax.random.randint(jax.random.fold_in(own, 2), (rows, 1), 0, top)
    return jnp.take_along_axis(listing, (jnp.arange(top)[None, :] + turn) % top, axis=1)


def shares(amount, total, bound, lean, full):
    weights = [(1 << 20) // math.isqrt(standing ** lean) + 1 for standing in range(1, amount + 1)]
    largest = bound if full else min(bound, max(-(-total // amount), total * weights[0] // sum(weights)))
    least = 1 if total - largest >= amount - 1 else 0
    given, rest = [largest] + [least] * (amount - 1), total - largest - least * (amount - 1)
    while rest > 0:
        candidates = [i for i in range(1, amount) if given[i] < largest] or [i for i in range(1, amount) if given[i] < bound]
        mass, left = sum([weights[i] for i in candidates]), rest
        for i in candidates:
            extra = min(bound - given[i], max(1, left * weights[i] // mass), rest)
            given[i] = given[i] + extra
            rest = rest - extra
    return np.array(given)


def bell_draw(key, dims, scale, bound, cuts=(), kind=jnp.bfloat16):
    factor_of = level_of(key, dims, cuts, -0.22, 0.18) if cuts else 1.0
    result = jax.random.normal(key, dims, jnp.float32) * scale * factor_of
    return jnp.minimum(jnp.maximum(result, -bound), bound).astype(kind)


def setup_inputs(seed: int = 0, part: int = 0) -> dict:
    seeds = jax.random.split(jax.random.key(seed), 9)
    part_cycle = touch_ends(jax.random.randint(seeds[0], (N_SHELL, TILES_ROW, PART_TILE), 0, CYCLE_DEV), jax.random.fold_in(seeds[0], 1), 0, CYCLE_DEV - 1).astype(jnp.int32)
    part_pixel = touch_ends(jax.random.randint(seeds[1], (N_SHELL, TILES_ROW, PART_TILE), 0, TP), jax.random.fold_in(seeds[1], 1), 0, TP - 1).astype(jnp.int32)
    part_mass = jnp.clip(jnp.exp(math.log(3.0) - 2.3025851 * jax.random.uniform(seeds[2], (N_SHELL, TILES_ROW, PART_TILE), jnp.float32) ** level_of(seeds[2], (N_SHELL, TILES_ROW, PART_TILE), ((0, 2), (1, 8)), -0.2, 0.2)), 0.3, 3.0)
    tile_block_keys = jax.random.split(jax.random.fold_in(seeds[3], 1), N_SHELL * TILES_ROW // TILES_DEV)
    tile_block_turns = jax.random.permutation(jax.random.fold_in(seeds[3], 3), N_SHELL * TILES_ROW // TILES_DEV)
    tile_block = jax.vmap(lambda own, number: deal_out(jax.random.fold_in(seeds[3], 2), own, number, TILES_DEV, BLOCKS, 1, CAP, 2))(tile_block_keys, tile_block_turns).reshape((N_SHELL, TILES_ROW, 1))
    tile_shell = touch_ends(jax.random.randint(seeds[4], (N_SHELL, TILES_ROW), 0, SHELL_DEV), jax.random.fold_in(seeds[4], 1), 0, SHELL_DEV - 1).astype(jnp.int32)
    tile_pixel = touch_ends(jax.random.randint(seeds[5], (N_SHELL, TILES_ROW), 0, NBLK), jax.random.fold_in(seeds[5], 1), 0, NBLK - 1).astype(jnp.int32)
    harmonic_basis = bell_draw(seeds[6], (M, CYCLES, L), CYCLES ** -0.5, 1.5, ((0, 4), (1, 2)))
    lens_weight = jnp.clip(jnp.exp(jax.random.uniform(seeds[7], (SOURCES, SHELLS), jnp.float32, math.log(0.2), math.log(1.0))), 0.2, 1.0)
    return dict(part_cycle=part_cycle, part_pixel=part_pixel, part_mass=part_mass, tile_block=tile_block, tile_shell=tile_shell, tile_pixel=tile_pixel, harmonic_basis=harmonic_basis, lens_weight=lens_weight)


precise = lax.Precision.HIGHEST


def deposit(cycle_index, pixel_index, masses):
    cycle_axis = jnp.arange(CYCLE_DEV, dtype=jnp.float32)
    pixel_axis = jnp.arange(TP, dtype=jnp.float32)
    cycle_part = jnp.exp(-0.5 * (cycle_axis[None, None, :] - cycle_index.astype(jnp.float32)[:, :, None]) ** 2)
    pixel_part = jnp.exp(-(pixel_axis[None, None, :] - pixel_index.astype(jnp.float32)[:, :, None]) ** 2 / 18.0)
    weighted = pixel_part * masses[:, :, None]
    return jnp.einsum("tpk,tpj->tkj", cycle_part, weighted, precision=precise)


def fourier_table():
    pixels = jnp.arange(NP, dtype=jnp.int32)
    orders = jnp.arange(M, dtype=jnp.int32)
    phases = (pixels[:, None] * orders[None, :]) % NP
    angles = phases.astype(jnp.float32) * (2.0 * math.pi / NP)
    return jnp.concatenate([jnp.cos(angles), -jnp.sin(angles)], axis=1)


def deposit_block(packed):
    return deposit(packed[0], packed[1], packed[2])


def reference(part_cycle, part_pixel, part_mass, tile_block, tile_shell, tile_pixel, harmonic_basis, lens_weight):
    row_tiles = part_cycle.shape[1]
    tile_count = part_cycle.shape[0] * row_tiles
    cycle_flat = part_cycle.reshape(tile_count // TILES_DEV, TILES_DEV, PART_TILE)
    pixel_flat = part_pixel.reshape(tile_count // TILES_DEV, TILES_DEV, PART_TILE)
    mass_flat = part_mass.reshape(tile_count // TILES_DEV, TILES_DEV, PART_TILE)
    tile_sums = lax.map(deposit_block, (cycle_flat, pixel_flat, mass_flat)).reshape(tile_count, CYCLE_DEV, TP)
    group_of = jnp.arange(tile_count, dtype=jnp.int32) // row_tiles
    shell_of = (group_of * SHELL_DEV + tile_shell.reshape(tile_count)).astype(jnp.int32)
    block_of = tile_block.reshape(tile_count).astype(jnp.int32)
    pixel_of = tile_pixel.reshape(tile_count).astype(jnp.int32)
    sky_map = jnp.zeros((SHELLS, BLOCKS, CYCLE_DEV, NBLK, TP), jnp.float32)
    sky_map = sky_map.at[shell_of, block_of, :, pixel_of, :].add(tile_sums)
    flat_map = sky_map.reshape(SHELLS * CYCLES, NP)
    cycle_modes = jnp.dot(flat_map, fourier_table(), precision=precise) * (2.0 * math.pi / NP)
    cycle_modes = cycle_modes.astype(jnp.bfloat16).reshape(SHELLS, CYCLES, 2, M)
    harmonics = jnp.einsum("mrl,srcm->smcl", harmonic_basis.astype(jnp.float32), cycle_modes.astype(jnp.float32), precision=precise)
    source_ids = jnp.arange(SHELLS, dtype=jnp.int32)
    weights = lens_weight * (source_ids[None, :] <= source_ids[:, None]).astype(jnp.float32)
    return jnp.einsum("js,smcl->jmcl", weights, harmonics, precision=precise)
```

```python
import functools
import math

import jax
import jax.numpy as jnp
import numpy as np
from jax import lax
from jax.experimental import pallas as pl
from jax.experimental.pallas import tpu as pltpu
from jax.sharding import PartitionSpec as P

NP = 8192
M = 128
TP = 128
CYCLE_DEV = 2
SHELL_DEV = 2

f32 = jnp.float32
bf16 = jnp.bfloat16


def split(x):
    high = x.astype(bf16)
    return high, (x - high.astype(f32)).astype(bf16)


def dot(a, b, contract=((1,), (0,))):
    return lax.dot_general(a, b, (contract, ((), ())), preferred_element_type=f32)


def split_np(x):
    high = x.astype(np.float32).astype(bf16)
    return np.stack([high, (x - high.astype(np.float64)).astype(np.float32).astype(bf16)])


@functools.cache
def tables(sky):
    part = np.tile(np.arange(2), M)
    order = np.repeat(np.arange(M), 2)
    pixel = np.arange(TP)
    spread = np.exp(-((pixel[:, None] - pixel[None, :]) ** 2) / 18.0)
    angle = (pixel[:, None] * order[None, :] % NP) * (2.0 * math.pi / NP)
    wave = np.where(part == 0, np.cos(angle), -np.sin(angle))
    other = np.where(part == 0, -np.sin(angle), np.cos(angle))
    modes = split_np(spread @ np.concatenate([wave, other], 1))
    place = np.arange(NP // TP)
    turn = (place[:, None] * TP * order[None, :] % NP) * (2.0 * math.pi / NP)
    cosine, sine = np.cos(turn), -np.sin(turn)
    phase = split_np(np.concatenate([cosine, np.where(part == 0, -sine, sine)], 1))
    return modes, phase


def deposit_kernel(cyc, pix, mass, block, shell, place, modes_tab, phase_tab, out, h, *, blocks):
    tiles, count = cyc.shape[1:]
    columns = 2 * M
    faint = math.exp(-0.5)
    rows = lax.broadcasted_iota(jnp.int32, (TP, count), 0)
    row = lax.broadcasted_iota(jnp.int32, (8, TP), 0)

    def group(g, carry):
        at = pl.ds(pl.multiple_of(g * 8, 8), 8)
        c8, x8, m8 = cyc[0, at, :], pix[0, at, :], mass[0, at, :]
        far = m8 * faint
        w0, w1 = jnp.where(c8 == 0, m8, far), jnp.where(c8 == 0, far, m8)
        a0, b0 = split(w0)
        a1, b1 = split(w1)
        left = jnp.concatenate([x.astype(f32) for x in (a0, a1, b0, b1)], 0).astype(bf16)
        h0 = jnp.zeros((8, TP), f32)
        h1 = jnp.zeros((8, TP), f32)
        for t in range(8):
            hot = jnp.where(rows == x8[t : t + 1, :], 1.0, 0.0).astype(bf16)
            got = dot(left, hot, ((1,), (1,)))
            h0 = jnp.where(row == t, got[0:8] + got[16:24], h0)
            h1 = jnp.where(row == t, got[8:16] + got[24:32], h1)
        h[0, at, :] = h0
        h[1, at, :] = h1
        return carry

    lax.fori_loop(0, tiles // 8, group, 0)

    places = phase_tab.shape[1]
    hot_place = jnp.where(
        lax.broadcasted_iota(jnp.int32, (places, tiles), 0) == place[...], 1.0, 0.0
    ).astype(bf16)
    phase = dot(hot_place, phase_tab[0], ((0,), (0,))) + dot(hot_place, phase_tab[1], ((0,), (0,)))
    bins = SHELL_DEV * blocks
    key = shell[...] * blocks + block[...]
    hot_bin = jnp.where(
        lax.broadcasted_iota(jnp.int32, (bins, tiles), 0) == key, 1.0, 0.0
    ).astype(bf16)
    for k in range(CYCLE_DEV):
        high, low = split(h[k])
        modes = dot(high, modes_tab[0]) + dot(high, modes_tab[1]) + dot(low, modes_tab[0])
        turned = modes[:, :columns] * phase[:, :columns] + modes[:, columns:] * phase[:, columns:]
        high, low = split(turned)
        out[k] = dot(hot_bin, high) + dot(hot_bin, low)


def legendre_kernel(where, recv, weight, own, other, out, left, *, blocks):
    lanes = recv.shape[-1]
    orders = own.shape[0]
    cycles = own.shape[1]
    width = orders * cycles
    half = lanes // CYCLE_DEV
    planes = out.shape[0]

    @pl.when(pl.program_id(0) == 0)
    def _():
        sub, first = where[0], where[1] * planes
        maps = []
        for x in range(recv.shape[0]):
            total = recv[x, 0]
            for i in range(1, recv.shape[1]):
                total = total + recv[x, i]
            total = (total * (2.0 * math.pi / NP)).astype(bf16).astype(f32)
            maps += [total[s * blocks : (s + 1) * blocks] for s in range(SHELL_DEV)]
        column = lax.broadcasted_iota(jnp.int32, (blocks, width), 1)
        row = lax.broadcasted_iota(jnp.int32, (blocks, width), 0)
        wide = lax.broadcasted_iota(jnp.int32, (half, width), 1)
        keep = lax.broadcasted_iota(jnp.int32, (half, width), 0) // 2 == wide // cycles
        even = wide % CYCLE_DEV == 0
        for side in range(2):
            mine = sub if side == 0 else 1 - sub
            cycle = mine * cycles + column % cycles
            spread = jnp.where(row == cycle // CYCLE_DEV, 1.0, 0.0).astype(bf16)
            for i in range(planes):
                total = jnp.zeros((blocks, lanes), f32)
                for s, value in enumerate(maps):
                    factor = jnp.where(s <= first + i, weight[first + i, s], 0.0)
                    total = total + factor * value
                high, low = split(total)
                for j, piece in enumerate((high, low)):
                    grown = dot(piece, spread, ((0,), (0,)))
                    grown = jnp.where(even, grown[:half], grown[half:])
                    grown = jnp.where(keep, grown, 0.0).astype(bf16)
                    start = (j * planes + i) * half
                    left[side, start : start + half, :] = grown

    span = out.shape[-1]
    a = own[...].reshape(width, span)
    b = other[...].reshape(width, span)
    result = dot(left[0], a) + dot(left[1], b)
    result = result[: planes * half] + result[planes * half :]
    for i in range(planes):
        for m in range(orders):
            start = i * half + m * 2
            out[i, m, :, :] = result[start : start + 2, :]


def body(part_cycle, part_pixel, part_mass, tile_block, tile_shell, tile_pixel, basis, lens_weight):
    sky, sub, shells = lax.axis_size("sky"), lax.axis_size("sub"), lax.axis_size("shell")
    tiles, count = part_cycle.shape[1:]
    orders, cycles, degrees = basis.shape
    blocks = cycles * sub // CYCLE_DEV
    sources = lens_weight.shape[0] // shells
    columns = 2 * M
    modes_tab, phase_tab = tables(sky)

    other = lax.ppermute(basis, "sub", [(i, (i + 1) % sub) for i in range(sub)])

    binned = pl.pallas_call(
        functools.partial(deposit_kernel, blocks=blocks),
        out_shape=jax.ShapeDtypeStruct((CYCLE_DEV, SHELL_DEV * blocks, columns), f32),
        scratch_shapes=[pltpu.VMEM((CYCLE_DEV, tiles, TP), f32)],
        name="deposit",
    )(
        part_cycle,
        part_pixel,
        part_mass,
        tile_block.reshape(1, tiles),
        tile_shell,
        tile_pixel,
        jnp.asarray(modes_tab),
        jnp.asarray(phase_tab),
    )
    lanes = CYCLE_DEV * orders * 2
    send = binned.reshape(CYCLE_DEV, SHELL_DEV * blocks, sky, orders * 2).transpose(2, 1, 0, 3)
    send = send.reshape(sky, 1, SHELL_DEV * blocks, lanes)
    send = jnp.broadcast_to(send, (sky, shells * sub, SHELL_DEV * blocks, lanes))
    send = send.reshape(sky * shells * sub, SHELL_DEV * blocks, lanes)
    recv = lax.all_to_all(send, ("sky", "shell", "sub"), 0, 0, tiled=True)
    recv = recv.reshape(sky, shells, sub, SHELL_DEV * blocks, lanes).transpose(1, 0, 2, 3, 4)
    recv = recv.reshape(shells, sky * sub, SHELL_DEV * blocks, lanes)

    where = jnp.stack([lax.axis_index("sub"), lax.axis_index("shell")]).astype(jnp.int32)
    own_degrees = degrees // sub
    span = min(own_degrees, 512)
    steps = own_degrees // span
    half = orders * 2
    return pl.pallas_call(
        functools.partial(legendre_kernel, blocks=blocks),
        out_shape=jax.ShapeDtypeStruct((sources, orders, 2, own_degrees), f32),
        grid_spec=pltpu.PrefetchScalarGridSpec(
            num_scalar_prefetch=1,
            grid=(steps,),
            in_specs=[
                pl.BlockSpec(recv.shape, lambda j, w: (0, 0, 0, 0)),
                pl.BlockSpec(memory_space=pltpu.SMEM),
                pl.BlockSpec((orders, cycles, span), lambda j, w: (0, 0, w[0] * steps + j)),
                pl.BlockSpec((orders, cycles, span), lambda j, w: (0, 0, w[0] * steps + j)),
            ],
            out_specs=pl.BlockSpec((sources, orders, 2, span), lambda j, w: (0, 0, 0, j)),
            scratch_shapes=[pltpu.VMEM((2, 2 * sources * half, orders * cycles), bf16)],
        ),
        name="legendre",
    )(where, recv, lens_weight, basis, other)


def solution(mesh):
    return jax.shard_map(
        body,
        mesh=mesh,
        in_specs=(
            P("shell", ("sky", "sub"), None),
            P("shell", ("sky", "sub"), None),
            P("shell", ("sky", "sub"), None),
            P("shell", ("sky", "sub"), None),
            P("shell", ("sky", "sub")),
            P("shell", ("sky", "sub")),
            P("sky", "sub", None),
            P(),
        ),
        out_specs=P(("groups", "shell"), "sky", None, "sub"),
        check_vma=False,
    )
```

```python
import functools
import math

import jax
import jax.numpy as jnp
import numpy as np
from jax import lax
from jax.experimental import pallas as pl
from jax.experimental.pallas import tpu as pltpu
from jax.sharding import PartitionSpec as P

NP = 8192
M = 128
TP = 128
CYCLE_DEV = 2
SHELL_DEV = 2

f32 = jnp.float32
bf16 = jnp.bfloat16


def split(x):
    high = x.astype(bf16)
    return high, (x - high.astype(f32)).astype(bf16)


def dot(a, b, contract=((1,), (0,))):
    return lax.dot_general(a, b, (contract, ((), ())), preferred_element_type=f32)


def split_np(x):
    high = x.astype(np.float32).astype(bf16)
    return np.stack([high, (x - high.astype(np.float64)).astype(np.float32).astype(bf16)])


@functools.cache
def tables():
    order = np.arange(M)
    pixel = np.arange(TP)
    spread = np.exp(-((pixel[:, None] - pixel[None, :]) ** 2) / 18.0)
    angle = (order[:, None] * pixel[None, :] % NP) * (2.0 * math.pi / NP)
    modes = split_np(np.concatenate([np.cos(angle), -np.sin(angle)], 0) @ spread)
    place = np.arange(NP // TP)
    turn = (order[:, None] * place[None, :] * TP % NP) * (2.0 * math.pi / NP)
    phase = split_np(np.concatenate([np.cos(turn), -np.sin(turn)], 0))
    return modes, phase


HIGH = 8
LOW = TP // HIGH


def histogram(cyc, pix, mass, start):
    count = cyc.shape[-1]
    faint = math.exp(-0.5)
    level = lax.broadcasted_iota(jnp.int32, (LOW, count), 0)
    lane = lax.broadcasted_iota(jnp.int32, (LOW, TP), 1)
    slot, tile = lane // 16, lane % 8
    none = jnp.zeros((16, count), bf16)
    sums = [jnp.zeros((LOW, TP), f32) for _ in range(HIGH)]
    for g in range(8):
        at = pl.ds(pl.multiple_of(start + g * 8, 8), 8)
        c8, x8, m8 = cyc[0, at, :], pix[0, at, :], mass[0, at, :]
        far = m8 * faint
        near = jnp.concatenate([jnp.where(c8 == 0, m8, far), jnp.where(c8 == 0, far, m8)], 0)
        pieces = split(near)
        top = x8 // LOW
        top = jnp.concatenate([top, top], 0).astype(jnp.int16)
        masks = [top == ((s - g) % HIGH) for s in range(8)]
        right = jnp.concatenate([jnp.where(k, p, none) for p in pieces for k in masks], 0)
        low = x8 % LOW
        left = [jnp.where(level == low[j : j + 1, :], 1.0, 0.0).astype(bf16) for j in range(8)]
        got = dot(jnp.concatenate(left, 0), right, ((1,), (1,)))
        got = got[:, :TP] + got[:, TP:]
        mine = got[:LOW]
        for j in range(1, 8):
            mine = jnp.where(tile == j, got[j * LOW : (j + 1) * LOW], mine)
        for s in range(8):
            e = (s - g) % HIGH
            sums[e] = jnp.where(slot == s, mine, sums[e])
    sums = [sums[0]] + [pltpu.roll(sums[e], TP - 16 * e, 1) for e in range(1, HIGH)]
    return jnp.concatenate(sums, 0)


def deposit_kernel(
    cyc_at, pix_at, mass_at, place_at, shell_at, block_at, modes_at, phase_at, basis, out, own,
    cyc, pix, mass, place, shell, block, modes_tab, phase_tab, h, phase, rot, row_sems, sems, *, blocks,
):
    tiles = cyc.shape[1]
    wide = CYCLE_DEV * tiles
    bins = SHELL_DEV * blocks
    parts = tiles // 64
    me = lax.axis_index("sky")

    def rows(part):
        at = pl.ds(part * 64, 64)
        pairs = ((cyc_at, cyc), (pix_at, pix), (mass_at, mass))
        return [
            pltpu.make_async_copy(a.at[:, at, :], b.at[:, at, :], row_sems.at[part, i])
            for i, (a, b) in enumerate(pairs)
        ]

    degrees = own.shape[2]
    near = pl.ds(pl.multiple_of(lax.axis_index("sub") * degrees, 128), degrees)
    pairs = ((place_at, place), (shell_at, shell), (block_at, block), (phase_at, phase_tab), (modes_at, modes_tab))
    pairs += ((basis.at[:, :, near], own),)
    small = [pltpu.make_async_copy(a, b, sems.at[i]) for i, (a, b) in enumerate(pairs)]
    for copy in small[:4] + [c for part in range(parts) for c in rows(part)] + small[4:]:
        copy.start()

    for copy in small[:4]:
        copy.wait()
    column = lax.broadcasted_iota(jnp.int32, (tiles, wide), 1)
    double = (column // 16) * 8 + column % 8 == lax.broadcasted_iota(jnp.int32, (tiles, wide), 0)
    double = jnp.where(double, 1.0, 0.0).astype(bf16)
    marks = jnp.concatenate([place[...], shell[...] * blocks + block[...]], 0)
    named = dot(marks.astype(f32).astype(bf16), double).astype(jnp.int32)
    places = phase_tab.shape[2]
    hot_place = lax.broadcasted_iota(jnp.int32, (places, wide), 0) == named[0:1]
    hot_place = jnp.where(hot_place, 1.0, 0.0).astype(bf16)
    phase[...] = dot(phase_tab[0], hot_place) + dot(phase_tab[1], hot_place)
    column = lax.broadcasted_iota(jnp.int32, (1, wide), 1)
    key = (column // 8 % CYCLE_DEV) * bins + named[1:2]
    hot_bin = lax.broadcasted_iota(jnp.int32, (CYCLE_DEV * bins, wide), 0) == key
    hot_bin = jnp.where(hot_bin, 1.0, 0.0).astype(bf16)

    for part in range(parts):
        for copy in rows(part):
            copy.wait()
        h[:, part * TP : (part + 1) * TP] = histogram(cyc, pix, mass, part * 64)

    small[4].wait()
    high, low = split(h[...])
    modes = dot(modes_tab[0], high) + dot(modes_tab[1], high) + dot(modes_tab[0], low)
    real, imag, cosine, sine = modes[:M], modes[M:], phase[:M, :], phase[M:, :]
    turned = real * cosine - imag * sine, real * sine + imag * cosine
    sums = jnp.zeros((CYCLE_DEV * bins, 2 * M), f32)
    for i in range(wide // TP):
        for j in range(2):
            rot[i, pl.ds(j, M, 2), :] = turned[j][:, i * TP : (i + 1) * TP]
    for i in range(wide // TP):
        left = hot_bin[:, i * TP : (i + 1) * TP]
        for piece in split(rot[i]):
            sums = sums + dot(left, piece, ((1,), (1,)))
    width = out.shape[-1] // CYCLE_DEV
    for z in range(out.shape[0]):
        out[me ^ z] = jnp.concatenate(
            [sums[k * bins : (k + 1) * bins, z * width : (z + 1) * width] for k in range(CYCLE_DEV)], 1
        )
    small[5].wait()


LIMIT = 24 << 20


def stages_of(sky, shells):
    bits = [("sub", 1)]
    bits += [("sky", 1 << i) for i in range(sky.bit_length() - 1)]
    bits += [("shell", 1 << i) for i in range(shells.bit_length() - 1)]
    return [[bit] for bit in bits]


AXES = ("sky", "shell", "sub")


def swap(x, change):
    sizes = [lax.axis_size(a) for a in AXES]
    pairs = []
    for here in np.ndindex(*sizes):
        there = [i ^ change.get(a, 0) for a, i in zip(AXES, here)]
        pairs.append((int(np.ravel_multi_index(here, sizes)), int(np.ravel_multi_index(there, sizes))))
    return lax.ppermute(x, AXES, pairs)


def exchange(y, stages):
    groups = {0: y}
    for number, steps in enumerate(stages):
        last = number == len(stages) - 1
        skies = [bit for axis, bit in steps if axis == "sky"]
        width = len(skies)
        fresh = {}
        for g, value in groups.items():
            rest = value.shape[1:]
            value = value.reshape((-1,) + (2,) * width + rest)
            for chosen in range(1 << len(steps)):
                change, index, target = {}, [slice(None)] + [0] * width, g
                for i, (axis, bit) in enumerate(steps):
                    if chosen >> i & 1:
                        change[axis] = change.get(axis, 0) ^ bit
                        if axis == "sky":
                            index[width - skies.index(bit)] = 1
                        if axis == "shell":
                            target ^= bit
                piece = value[tuple(index)]
                fresh.setdefault(target, []).append(swap(piece, change) if change else piece)
        if last:
            return [fresh[g] for g in sorted(fresh)]
        groups = {g: sum(pieces[1:], pieces[0]) for g, pieces in fresh.items()}


def legendre_kernel(weight, own, other, *refs, counts, blocks):
    refs, out, left = refs[:-2], refs[-2], refs[-1]
    lanes = refs[0].shape[-1]
    orders = own.shape[0]
    cycles = own.shape[1]
    width = orders * cycles
    half = lanes // CYCLE_DEV
    planes = out.shape[0]
    sub, place = lax.axis_index("sub"), lax.axis_index("shell")

    @pl.when(pl.program_id(0) == 0)
    def _():
        first = place * planes
        maps = []
        for x, count in enumerate(counts):
            at = sum(counts[:x])
            total = refs[at][0]
            for i in range(1, count):
                total = total + refs[at + i][0]
            total = (total * (2.0 * math.pi / NP)).astype(bf16).astype(f32)
            maps += [
                ((place ^ x) * SHELL_DEV + s, total[s * blocks : (s + 1) * blocks])
                for s in range(SHELL_DEV)
            ]
        column = lax.broadcasted_iota(jnp.int32, (blocks, width), 1)
        row = lax.broadcasted_iota(jnp.int32, (blocks, width), 0)
        wide = lax.broadcasted_iota(jnp.int32, (half, width), 1)
        keep = lax.broadcasted_iota(jnp.int32, (half, width), 0) // 2 == wide // cycles
        even = wide % CYCLE_DEV == 0
        for side in range(2):
            mine = sub if side == 0 else 1 - sub
            cycle = mine * cycles + column % cycles
            spread = jnp.where(row == cycle // CYCLE_DEV, 1.0, 0.0).astype(bf16)
            for i in range(planes):
                total = jnp.zeros((blocks, lanes), f32)
                for s, value in maps:
                    factor = jnp.where(s <= first + i, weight[first + i, s], 0.0)
                    total = total + factor * value
                high, low = split(total)
                for j, piece in enumerate((high, low)):
                    grown = dot(piece, spread, ((0,), (0,)))
                    grown = jnp.where(even, grown[:half], grown[half:])
                    grown = jnp.where(keep, grown, 0.0).astype(bf16)
                    start = (j * planes + i) * half
                    left[side, start : start + half, :] = grown

    span = out.shape[-1]
    start = pl.program_id(0) * span
    a = own[:, :, pl.ds(pl.multiple_of(start, 128), span)].reshape(width, span)
    start = start + sub * own.shape[2]
    b = other[:, :, pl.ds(pl.multiple_of(start, 128), span)].reshape(width, span)
    result = dot(left[0], a) + dot(left[1], b)
    result = result[: planes * half] + result[planes * half :]
    for i in range(planes):
        for m in range(orders):
            start = i * half + m * 2
            out[i, m, :, :] = result[start : start + 2, :]


def body(part_cycle, part_pixel, part_mass, tile_block, tile_shell, tile_pixel, basis, lens_weight):
    sky, sub, shells = lax.axis_size("sky"), lax.axis_size("sub"), lax.axis_size("shell")
    tiles, count = part_cycle.shape[1:]
    orders, cycles, degrees = basis.shape
    blocks = cycles * sub // CYCLE_DEV
    sources = lens_weight.shape[0] // shells
    modes_tab, phase_tab = (jnp.asarray(t) for t in tables())

    other = lax.ppermute(basis, "sub", [(i, (i + 1) % sub) for i in range(sub)])

    lanes = CYCLE_DEV * orders * 2
    bins = SHELL_DEV * blocks
    own_degrees = degrees // sub
    anywhere = pl.BlockSpec(memory_space=pltpu.HBM)
    vmem = pl.BlockSpec(memory_space=pltpu.VMEM)
    send, own = pl.pallas_call(
        functools.partial(deposit_kernel, blocks=blocks),
        out_shape=(
            jax.ShapeDtypeStruct((sky, bins, lanes), f32),
            jax.ShapeDtypeStruct((orders, cycles, own_degrees), bf16),
        ),
        in_specs=[anywhere] * 9,
        out_specs=(vmem, vmem),
        scratch_shapes=[
            pltpu.VMEM((1, tiles, count), jnp.int32),
            pltpu.VMEM((1, tiles, count), jnp.int32),
            pltpu.VMEM((1, tiles, count), f32),
            pltpu.VMEM((1, tiles), jnp.int32),
            pltpu.VMEM((1, tiles), jnp.int32),
            pltpu.VMEM((1, tiles), jnp.int32),
            pltpu.VMEM(modes_tab.shape, bf16),
            pltpu.VMEM(phase_tab.shape, bf16),
            pltpu.VMEM((TP, CYCLE_DEV * tiles), f32),
            pltpu.VMEM((2 * M, CYCLE_DEV * tiles), f32),
            pltpu.VMEM((CYCLE_DEV * tiles // TP, 2 * M, TP), f32),
            pltpu.SemaphoreType.DMA((tiles // 64, 3)),
            pltpu.SemaphoreType.DMA((6,)),
        ],
        compiler_params=pltpu.CompilerParams(vmem_limit_bytes=LIMIT),
        name="deposit",
    )(
        *(
            pltpu.with_memory_space_constraint(x, pltpu.HBM)
            for x in (
                part_cycle,
                part_pixel,
                part_mass,
                tile_pixel,
                tile_shell,
                tile_block.reshape(1, tiles),
                modes_tab,
                phase_tab,
                basis,
            )
        )
    )
    parts = exchange(send, stages_of(sky, shells))

    span = min(own_degrees, 512)
    half = orders * 2
    flat = [piece for group in parts for piece in group]
    return pl.pallas_call(
        functools.partial(legendre_kernel, counts=[len(group) for group in parts], blocks=blocks),
        out_shape=jax.ShapeDtypeStruct((sources, orders, 2, own_degrees), f32),
        grid=(own_degrees // span,),
        in_specs=[pl.BlockSpec(memory_space=pltpu.SMEM), vmem, vmem] + [vmem] * len(flat),
        out_specs=pl.BlockSpec((sources, orders, 2, span), lambda j: (0, 0, 0, j)),
        scratch_shapes=[pltpu.VMEM((2, 2 * sources * half, orders * cycles), bf16)],
        compiler_params=pltpu.CompilerParams(vmem_limit_bytes=LIMIT),
        name="legendre",
    )(lens_weight, own, other, *flat)


def solution(mesh):
    return jax.shard_map(
        body,
        mesh=mesh,
        in_specs=(
            P("shell", ("sky", "sub"), None),
            P("shell", ("sky", "sub"), None),
            P("shell", ("sky", "sub"), None),
            P("shell", ("sky", "sub"), None),
            P("shell", ("sky", "sub")),
            P("shell", ("sky", "sub")),
            P("sky", "sub", None),
            P(),
        ),
        out_specs=P(("groups", "shell"), "sky", None, "sub"),
        check_vma=False,
    )
```

```python
import functools
import math

import jax
import jax.numpy as jnp
import numpy as np
from jax import lax
from jax.experimental import pallas as pl
from jax.experimental.pallas import tpu as pltpu
from jax.sharding import PartitionSpec as P

NP = 8192
M = 128
TP = 128
CYCLE_DEV = 2
SHELL_DEV = 2

f32 = jnp.float32
bf16 = jnp.bfloat16


def split(x):
    high = x.astype(bf16)
    return high, (x - high.astype(f32)).astype(bf16)


def dot(a, b, contract=((1,), (0,))):
    return lax.dot_general(a, b, (contract, ((), ())), preferred_element_type=f32)


def split_np(x):
    high = x.astype(np.float32).astype(bf16)
    return np.concatenate([high, (x - high.astype(np.float64)).astype(np.float32).astype(bf16)], 1)


@functools.cache
def tables():
    order = np.arange(M)
    pixel = np.arange(TP)
    spread = np.exp(-((pixel[:, None] - pixel[None, :]) ** 2) / 18.0)
    angle = (order[:, None] * pixel[None, :] % NP) * (2.0 * math.pi / NP)
    modes = split_np(np.concatenate([np.cos(angle), -np.sin(angle)], 0) @ spread)
    place = np.arange(NP // TP)
    turn = (order[:, None] * place[None, :] * TP % NP) * (2.0 * math.pi / NP)
    phase = split_np(np.concatenate([np.cos(turn), -np.sin(turn)], 0))
    return modes, phase


HIGH = 8
LOW = TP // HIGH
GROUP = 4
SHIFT = LOW.bit_length() - 1


def histogram(cyc, pix, mass, start):
    count = cyc.shape[-1]
    level = lax.broadcasted_iota(jnp.int16, (LOW, count), 0)
    lane = lax.broadcasted_iota(jnp.int32, (LOW, TP), 1)
    slot, tile = lane >> 4, lane & 7
    one, none = jnp.ones((LOW, count), bf16), jnp.zeros((16, count), bf16)
    sums = [jnp.zeros((LOW, TP), f32) for _ in range(HIGH)]
    for g in range(8):
        at = pl.ds(start + g * 8, 8)
        c8, x8, m8 = cyc[0, at, :], pix[0, at, :], mass[0, at, :]
        top = x8 >> SHIFT
        first = jnp.where(c8 == 0, top, HIGH)
        other = jnp.where(c8 == 0, HIGH, top)
        top = jnp.concatenate([first, other], 0).astype(jnp.int16)
        masks = [top == (s - g) % HIGH for s in range(8)]
        pieces = split(jnp.concatenate([m8, m8], 0))
        right = jnp.concatenate([jnp.where(k, p, none) for p in pieces for k in masks], 0)
        low = (x8 & (LOW - 1)).astype(jnp.int16)
        left = [jnp.where(level == low[j : j + 1, :], one, none) for j in range(8)]
        got = dot(jnp.concatenate(left, 0), right, ((1,), (1,)))
        got = got[:, :TP] + got[:, TP:]
        mine = got[:LOW]
        for j in range(1, 8):
            mine = jnp.where(tile == j, got[j * LOW : (j + 1) * LOW], mine)
        for s in range(8):
            e = (s - g) % HIGH
            sums[e] = jnp.where(slot == s, mine, sums[e])
    sums = [sums[0]] + [pltpu.roll(sums[e], TP - 16 * e, 1) for e in range(1, HIGH)]
    return jnp.concatenate(sums, 0)


def deposit_kernel(
    cyc_at, pix_at, mass_at, place_at, shell_at, block_at, modes_at, phase_at, basis, out, own,
    cyc, pix, mass, place, shell, block, modes_tab, phase_tab, rot, row_sems, sems, *, blocks,
):
    tiles = cyc.shape[1]
    wide = CYCLE_DEV * tiles
    bins = SHELL_DEV * blocks
    parts = tiles // 64
    me = lax.axis_index("sky")

    def rows(part):
        at = pl.ds(part * 64, 64)
        pairs = ((cyc_at, cyc), (pix_at, pix), (mass_at, mass))
        return [
            pltpu.make_async_copy(a.at[:, at, :], b.at[:, at, :], row_sems.at[part, i])
            for i, (a, b) in enumerate(pairs)
        ]

    degrees = own.shape[2]
    near = pl.ds(pl.multiple_of(lax.axis_index("sub") * degrees, 128), degrees)
    pairs = ((place_at, place), (shell_at, shell), (block_at, block), (phase_at, phase_tab), (modes_at, modes_tab))
    pairs += ((basis.at[:, :, near], own),)
    small = [pltpu.make_async_copy(a, b, sems.at[i]) for i, (a, b) in enumerate(pairs)]
    for copy in [c for part in range(parts) for c in rows(part)] + small:
        copy.start()

    for copy in [c for part in range(parts) for c in rows(part)] + small[:5]:
        copy.wait()
    column = lax.broadcasted_iota(jnp.int32, (64, TP), 1)
    double = ((column >> 4) << 3) + (column & 7) == lax.broadcasted_iota(jnp.int32, (64, TP), 0)
    double = jnp.where(double, 1.0, 0.0).astype(bf16)
    marks = jnp.concatenate([place[...], shell[...] * blocks + block[...]], 0).astype(f32).astype(bf16)
    named = [dot(marks[:, part * 64 : (part + 1) * 64], double) for part in range(parts)]
    named = jnp.concatenate(named, 1).astype(jnp.int32)
    places = phase_tab.shape[1] // 2
    hot_place = lax.broadcasted_iota(jnp.int32, (places, wide), 0) == named[0:1]
    hot_place = jnp.where(hot_place, 1.0, 0.0).astype(bf16)
    column = lax.broadcasted_iota(jnp.int32, (1, wide), 1)
    key = ((column >> 3) & 1) * bins + named[1:2]
    hot_bin = lax.broadcasted_iota(jnp.int32, (CYCLE_DEV * bins, wide), 0) == key
    hot_bin = jnp.where(hot_bin, 1.0, 0.0).astype(bf16)

    sums = jnp.zeros((CYCLE_DEV * bins, 2 * M), f32)
    for part in range(0, parts, GROUP):
        at = slice(part * TP, (part + GROUP) * TP)
        h = [histogram(cyc, pix, mass, i * 64) for i in range(part, part + GROUP)]
        phase = dot(phase_tab[...], jnp.concatenate([hot_place, hot_place], 0))
        high, low = split(jnp.concatenate(h, 1))
        modes = dot(modes_tab[...], jnp.concatenate([high, high], 0)) + dot(modes_tab[:, :TP], low)
        real, imag, cosine, sine = modes[:M], modes[M:], phase[:M, at], phase[M:, at]
        turned = real * cosine - imag * sine, real * sine + imag * cosine
        for i in range(GROUP):
            for j in range(2):
                rot[part + i, pl.ds(j, M, 2), :] = turned[j][:, i * TP : (i + 1) * TP]
        pieces = [split(rot[part + i]) for i in range(GROUP)]
        for j in range(2):
            right = jnp.concatenate([p[j] for p in pieces], 1)
            sums = sums + dot(hot_bin[:, at], right, ((1,), (1,)))
    faint = math.exp(-0.5)
    sums = sums + faint * jnp.concatenate([sums[bins:], sums[:bins]], 0)
    width = out.shape[-1] // CYCLE_DEV
    for z in range(out.shape[0]):
        out[me ^ z] = jnp.concatenate(
            [sums[k * bins : (k + 1) * bins, z * width : (z + 1) * width] for k in range(CYCLE_DEV)], 1
        )
    small[5].wait()


LIMIT = 24 << 20
SPAN = 512


def stages_of(sky, shells):
    bits = [("sub", 1)]
    bits += [("sky", 1 << i) for i in range(sky.bit_length() - 1)]
    bits += [("shell", 1 << i) for i in range(shells.bit_length() - 1)]
    return [[bit] for bit in bits]


AXES = ("sky", "shell", "sub")


def swap(x, change):
    sizes = [lax.axis_size(a) for a in AXES]
    pairs = []
    for here in np.ndindex(*sizes):
        there = [i ^ change.get(a, 0) for a, i in zip(AXES, here)]
        pairs.append((int(np.ravel_multi_index(here, sizes)), int(np.ravel_multi_index(there, sizes))))
    return lax.ppermute(x, AXES, pairs)


def exchange(y, stages):
    groups = {0: y}
    for number, steps in enumerate(stages):
        last = number == len(stages) - 1
        skies = [bit for axis, bit in steps if axis == "sky"]
        width = len(skies)
        fresh = {}
        for g, value in groups.items():
            rest = value.shape[1:]
            value = value.reshape((-1,) + (2,) * width + rest)
            for chosen in range(1 << len(steps)):
                change, index, target = {}, [slice(None)] + [0] * width, g
                for i, (axis, bit) in enumerate(steps):
                    if chosen >> i & 1:
                        change[axis] = change.get(axis, 0) ^ bit
                        if axis == "sky":
                            index[width - skies.index(bit)] = 1
                        if axis == "shell":
                            target ^= bit
                piece = value[tuple(index)]
                fresh.setdefault(target, []).append(swap(piece, change) if change else piece)
        if last:
            return [fresh[g] for g in sorted(fresh)]
        groups = {g: sum(pieces[1:], pieces[0]) for g, pieces in fresh.items()}


def legendre_kernel(weight, own, other, *refs, counts, blocks):
    refs, (out, left, result, sems) = refs[:-4], refs[-4:]
    lanes = refs[0].shape[-1]
    orders = own.shape[0]
    cycles = own.shape[1]
    width = orders * cycles
    half = lanes // CYCLE_DEV
    planes = result.shape[0]
    sub, place = lax.axis_index("sub"), lax.axis_index("shell")

    first = place * planes
    maps = []
    for x, count in enumerate(counts):
        at = sum(counts[:x])
        total = refs[at][0]
        for i in range(1, count):
            total = total + refs[at + i][0]
        total = (total * (2.0 * math.pi / NP)).astype(bf16).astype(f32)
        maps += [
            ((place ^ x) * SHELL_DEV + s, total[s * blocks : (s + 1) * blocks])
            for s in range(SHELL_DEV)
        ]
    column = lax.broadcasted_iota(jnp.int32, (blocks, width), 1)
    row = lax.broadcasted_iota(jnp.int32, (blocks, width), 0)
    wide = lax.broadcasted_iota(jnp.int32, (half, width), 1)
    keep = lax.broadcasted_iota(jnp.int32, (half, width), 0) // 2 == wide // cycles
    even = wide % CYCLE_DEV == 0
    for side in range(2):
        mine = sub if side == 0 else 1 - sub
        cycle = mine * cycles + column % cycles
        spread = jnp.where(row == cycle // CYCLE_DEV, 1.0, 0.0).astype(bf16)
        for i in range(planes):
            total = jnp.zeros((blocks, lanes), f32)
            for s, value in maps:
                factor = jnp.where(s <= first + i, weight[first + i, s], 0.0)
                total = total + factor * value
            high, low = split(total)
            for j, piece in enumerate((high, low)):
                grown = dot(piece, spread, ((0,), (0,)))
                grown = jnp.where(even, grown[:half], grown[half:])
                grown = jnp.where(keep, grown, 0.0).astype(bf16)
                start = (j * planes + i) * half
                left[side, start : start + half, :] = grown

    copies = []
    for step in range(own.shape[2] // SPAN):
        at = pl.ds(step * SPAN, SPAN)
        far = pl.ds(pl.multiple_of(sub * own.shape[2] + step * SPAN, 128), SPAN)
        a = own[:, :, at].reshape(width, SPAN)
        b = other[:, :, far].reshape(width, SPAN)
        value = dot(left[0], a) + dot(left[1], b)
        value = value[: planes * half] + value[planes * half :]
        for i in range(planes):
            for m in range(orders):
                start = i * half + m * 2
                result[i, m, :, at] = value[start : start + 2, :]
        copies.append(pltpu.make_async_copy(result.at[:, :, :, at], out.at[:, :, :, at], sems.at[step]))
        copies[-1].start()
    for copy in copies:
        copy.wait()


def deposit_call(part_cycle, part_pixel, part_mass, place, shell, block, basis, sky, blocks, own_degrees):
    tiles, count = part_cycle.shape[1:]
    orders, cycles, _ = basis.shape
    lanes = CYCLE_DEV * orders * 2
    bins = SHELL_DEV * blocks
    modes_tab, phase_tab = (jnp.asarray(t) for t in tables())
    anywhere = pl.BlockSpec(memory_space=pltpu.HBM)
    vmem = pl.BlockSpec(memory_space=pltpu.VMEM)
    return pl.pallas_call(
        functools.partial(deposit_kernel, blocks=blocks),
        out_shape=(
            jax.ShapeDtypeStruct((sky, bins, lanes), f32),
            jax.ShapeDtypeStruct((orders, cycles, own_degrees), bf16),
        ),
        in_specs=[anywhere] * 9,
        out_specs=(vmem, vmem),
        scratch_shapes=[
            pltpu.VMEM((1, tiles, count), jnp.int32),
            pltpu.VMEM((1, tiles, count), jnp.int32),
            pltpu.VMEM((1, tiles, count), f32),
            pltpu.VMEM((1, tiles), jnp.int32),
            pltpu.VMEM((1, tiles), jnp.int32),
            pltpu.VMEM((1, tiles), jnp.int32),
            pltpu.VMEM(modes_tab.shape, bf16),
            pltpu.VMEM(phase_tab.shape, bf16),
            pltpu.VMEM((CYCLE_DEV * tiles // TP, 2 * M, TP), f32),
            pltpu.SemaphoreType.DMA((tiles // 64, 3)),
            pltpu.SemaphoreType.DMA((6,)),
        ],
        compiler_params=pltpu.CompilerParams(vmem_limit_bytes=LIMIT),
        name="deposit",
    )(
        *(
            pltpu.with_memory_space_constraint(x, pltpu.HBM)
            for x in (
                part_cycle,
                part_pixel,
                part_mass,
                place,
                shell,
                block,
                modes_tab,
                phase_tab,
                basis,
            )
        )
    )


def legendre_call(lens_weight, own, other, parts, planes, blocks):
    orders, cycles, degrees = own.shape
    flat = [piece for group in parts for piece in group]
    vmem = pl.BlockSpec(memory_space=pltpu.VMEM)
    return pl.pallas_call(
        functools.partial(legendre_kernel, counts=[len(group) for group in parts], blocks=blocks),
        out_shape=jax.ShapeDtypeStruct((planes, orders, 2, degrees), f32),
        in_specs=[pl.BlockSpec(memory_space=pltpu.SMEM), vmem, vmem] + [vmem] * len(flat),
        out_specs=pl.BlockSpec(memory_space=pltpu.HBM),
        scratch_shapes=[
            pltpu.VMEM((2, 4 * planes * orders, orders * cycles), bf16),
            pltpu.VMEM((planes, orders, 2, degrees), f32),
            pltpu.SemaphoreType.DMA((degrees // SPAN,)),
        ],
        compiler_params=pltpu.CompilerParams(vmem_limit_bytes=LIMIT),
        name="legendre",
    )(lens_weight, own, other, *flat)


def body(part_cycle, part_pixel, part_mass, tile_block, tile_shell, tile_pixel, basis, lens_weight):
    sky, sub, shells = lax.axis_size("sky"), lax.axis_size("sub"), lax.axis_size("shell")
    tiles = part_cycle.shape[1]
    _, cycles, degrees = basis.shape
    blocks = cycles * sub // CYCLE_DEV
    other = lax.ppermute(basis, "sub", [(i, (i + 1) % sub) for i in range(sub)])
    send, own = deposit_call(
        part_cycle,
        part_pixel,
        part_mass,
        tile_pixel,
        tile_shell,
        tile_block.reshape(1, tiles),
        basis,
        sky,
        blocks,
        degrees // sub,
    )
    parts = exchange(send, stages_of(sky, shells))
    return legendre_call(lens_weight, own, other, parts, lens_weight.shape[0] // shells, blocks)


def solution(mesh):
    return jax.shard_map(
        body,
        mesh=mesh,
        in_specs=(
            P("shell", ("sky", "sub"), None),
            P("shell", ("sky", "sub"), None),
            P("shell", ("sky", "sub"), None),
            P("shell", ("sky", "sub"), None),
            P("shell", ("sky", "sub")),
            P("shell", ("sky", "sub")),
            P("sky", "sub", None),
            P(),
        ),
        out_specs=P(("groups", "shell"), "sky", None, "sub"),
        check_vma=False,
    )
```

```python
import functools
import math

import jax
import jax.numpy as jnp
import numpy as np
from jax import lax
from jax.experimental import pallas as pl
from jax.experimental.pallas import tpu as pltpu
from jax.sharding import PartitionSpec as P


NP = 8192
M = 128
TP = 128
CYCLE_DEV = 2
SHELL_DEV = 2

f32 = jnp.float32
bf16 = jnp.bfloat16


def split(x):
    high = x.astype(bf16)
    return high, (x - high.astype(f32)).astype(bf16)


def dot(a, b, contract=((1,), (0,))):
    return lax.dot_general(a, b, (contract, ((), ())), preferred_element_type=f32)


def split_np(x):
    high = x.astype(np.float32).astype(bf16)
    return np.concatenate([high, (x - high.astype(np.float64)).astype(np.float32).astype(bf16)], 1)


@functools.cache
def tables():
    order = np.arange(M)
    pixel = np.arange(TP)
    spread = np.exp(-((pixel[:, None] - pixel[None, :]) ** 2) / 18.0)
    angle = (order[:, None] * pixel[None, :] % NP) * (2.0 * math.pi / NP)
    modes = split_np(np.concatenate([np.cos(angle), -np.sin(angle)], 0) @ spread)
    place = np.arange(NP // TP)
    turn = (order[:, None] * place[None, :] * TP % NP) * (2.0 * math.pi / NP)
    phase = split_np(np.concatenate([np.cos(turn), -np.sin(turn)], 0))
    return modes, phase


HIGH = 8
LOW = TP // HIGH
GROUP = 4
SHIFT = LOW.bit_length() - 1


def histogram(cyc, pix, mass, start):
    count = cyc.shape[-1]
    level = lax.broadcasted_iota(jnp.int16, (LOW, count), 0)
    lane = lax.broadcasted_iota(jnp.int32, (LOW, TP), 1)
    slot, tile = lane >> 4, lane & 7
    one, none = jnp.ones((LOW, count), bf16), jnp.zeros((16, count), bf16)
    sums = [jnp.zeros((LOW, TP), f32) for _ in range(HIGH)]
    for g in range(8):
        at = pl.ds(start + g * 8, 8)
        c8, x8, m8 = cyc[0, at, :], pix[0, at, :], mass[0, at, :]
        top = x8 >> SHIFT
        first = jnp.where(c8 == 0, top, HIGH)
        other = jnp.where(c8 == 0, HIGH, top)
        top = jnp.concatenate([first, other], 0).astype(jnp.int16)
        masks = [top == (s - g) % HIGH for s in range(8)]
        pieces = split(jnp.concatenate([m8, m8], 0))
        right = jnp.concatenate([jnp.where(k, p, none) for p in pieces for k in masks], 0)
        low = (x8 & (LOW - 1)).astype(jnp.int16)
        left = [jnp.where(level == low[j : j + 1, :], one, none) for j in range(8)]
        got = dot(jnp.concatenate(left, 0), right, ((1,), (1,)))
        got = got[:, :TP] + got[:, TP:]
        mine = got[:LOW]
        for j in range(1, 8):
            mine = jnp.where(tile == j, got[j * LOW : (j + 1) * LOW], mine)
        for s in range(8):
            e = (s - g) % HIGH
            sums[e] = jnp.where(slot == s, mine, sums[e])
    sums = [sums[0]] + [pltpu.roll(sums[e], TP - 16 * e, 1) for e in range(1, HIGH)]
    return jnp.concatenate(sums, 0)


def deposit_kernel(
    cyc_at, pix_at, mass_at, place_at, shell_at, block_at, modes_at, phase_at, basis, out, own,
    cyc, pix, mass, place, shell, block, modes_tab, phase_tab, rot, row_sems, sems, *, blocks,
):
    tiles = cyc.shape[1]
    wide = CYCLE_DEV * tiles
    bins = SHELL_DEV * blocks
    parts = tiles // 64
    me = lax.axis_index("sky")

    def rows(part):
        at = pl.ds(part * 64, 64)
        pairs = ((cyc_at, cyc), (pix_at, pix), (mass_at, mass))
        return [
            pltpu.make_async_copy(a.at[:, at, :], b.at[:, at, :], row_sems.at[part, i])
            for i, (a, b) in enumerate(pairs)
        ]

    degrees = own.shape[2]
    near = pl.ds(pl.multiple_of(lax.axis_index("sub") * degrees, 128), degrees)
    pairs = ((place_at, place), (shell_at, shell), (block_at, block), (phase_at, phase_tab), (modes_at, modes_tab))
    pairs += ((basis.at[:, :, near], own),)
    small = [pltpu.make_async_copy(a, b, sems.at[i]) for i, (a, b) in enumerate(pairs)]
    for copy in [c for part in range(parts) for c in rows(part)] + small:
        copy.start()

    for copy in [c for part in range(parts) for c in rows(part)] + small[:5]:
        copy.wait()
    column = lax.broadcasted_iota(jnp.int32, (64, TP), 1)
    double = ((column >> 4) << 3) + (column & 7) == lax.broadcasted_iota(jnp.int32, (64, TP), 0)
    double = jnp.where(double, 1.0, 0.0).astype(bf16)
    marks = jnp.concatenate([place[...], shell[...] * blocks + block[...]], 0).astype(f32).astype(bf16)
    named = [dot(marks[:, part * 64 : (part + 1) * 64], double) for part in range(parts)]
    named = jnp.concatenate(named, 1).astype(jnp.int32)
    places = phase_tab.shape[1] // 2
    hot_place = lax.broadcasted_iota(jnp.int32, (places, wide), 0) == named[0:1]
    hot_place = jnp.where(hot_place, 1.0, 0.0).astype(bf16)
    column = lax.broadcasted_iota(jnp.int32, (1, wide), 1)
    key = ((column >> 3) & 1) * bins + named[1:2]
    hot_bin = lax.broadcasted_iota(jnp.int32, (CYCLE_DEV * bins, wide), 0) == key
    hot_bin = jnp.where(hot_bin, 1.0, 0.0).astype(bf16)

    sums = jnp.zeros((CYCLE_DEV * bins, 2 * M), f32)
    for part in range(0, parts, GROUP):
        at = slice(part * TP, (part + GROUP) * TP)
        h = [histogram(cyc, pix, mass, i * 64) for i in range(part, part + GROUP)]
        phase = dot(phase_tab[...], jnp.concatenate([hot_place, hot_place], 0))
        high, low = split(jnp.concatenate(h, 1))
        modes = dot(modes_tab[...], jnp.concatenate([high, high], 0)) + dot(modes_tab[:, :TP], low)
        real, imag, cosine, sine = modes[:M], modes[M:], phase[:M, at], phase[M:, at]
        turned = real * cosine - imag * sine, real * sine + imag * cosine
        for i in range(GROUP):
            for j in range(2):
                rot[part + i, pl.ds(j, M, 2), :] = turned[j][:, i * TP : (i + 1) * TP]
        pieces = [split(rot[part + i]) for i in range(GROUP)]
        for j in range(2):
            right = jnp.concatenate([p[j] for p in pieces], 1)
            sums = sums + dot(hot_bin[:, at], right, ((1,), (1,)))
    faint = math.exp(-0.5)
    sums = sums + faint * jnp.concatenate([sums[bins:], sums[:bins]], 0)
    width = out.shape[-1] // CYCLE_DEV
    for z in range(out.shape[0]):
        out[me ^ z] = jnp.concatenate(
            [sums[k * bins : (k + 1) * bins, z * width : (z + 1) * width] for k in range(CYCLE_DEV)], 1
        )
    small[5].wait()


LIMIT = 24 << 20
SPAN = 512


AXES = ("sky", "shell", "sub")


def swap(x, change):
    sizes = [lax.axis_size(a) for a in AXES]
    pairs = []
    for here in np.ndindex(*sizes):
        there = [i ^ change.get(a, 0) for a, i in zip(AXES, here)]
        there[2] = sizes[2] - 1 - here[2]
        pairs.append((int(np.ravel_multi_index(here, sizes)), int(np.ravel_multi_index(there, sizes))))
    return lax.ppermute(x, AXES, pairs)


def exchange(y):
    y = y + swap(y, {})
    bit = 1
    while y.shape[0] > 1:
        y = y.reshape(-1, 2, *y.shape[1:])
        given = swap(y[:, 1], {"sky": bit})
        y = y[:, 0] + given
        bit *= 2
    parts, bit = [y], 1
    while bit < lax.axis_size("shell"):
        parts = parts + [swap(p, {"shell": bit}) for p in parts]
        bit *= 2
    return parts


def legendre_kernel(weight, own, other, *refs, blocks):
    refs, (out, left, result, sems) = refs[:-4], refs[-4:]
    orders, cycles, degrees = own.shape
    lanes = refs[0].shape[-1]
    planes = out.shape[0]
    some = orders // 2
    width = 2 * some * cycles
    sub, place = lax.axis_index("sub"), lax.axis_index("shell")

    first = place * planes
    maps = []
    for x, ref in enumerate(refs):
        total = (ref[0] * (2.0 * math.pi / NP)).astype(bf16).astype(f32)
        maps += [
            ((place ^ x) * SHELL_DEV + s, total[s * blocks : (s + 1) * blocks]) for s in range(SHELL_DEV)
        ]
    column = lax.broadcasted_iota(jnp.int32, (blocks, width), 1)
    row = lax.broadcasted_iota(jnp.int32, (blocks, width), 0)
    mine = jnp.where(column < width // 2, sub, 1 - sub)
    spread = jnp.where(row == (mine * cycles + column % cycles) // CYCLE_DEV, 1.0, 0.0).astype(bf16)
    half = 2 * some
    wide = lax.broadcasted_iota(jnp.int32, (half, width), 1)
    keep = lax.broadcasted_iota(jnp.int32, (half, width), 0) // 2 == wide % (width // 2) // cycles
    even = wide % CYCLE_DEV == 0
    for i in range(planes):
        total = jnp.zeros((blocks, lanes), f32)
        for s, value in maps:
            factor = jnp.where(s <= first + i, weight[first + i, s], 0.0)
            total = total + factor * value
        for j, piece in enumerate(split(total)):
            grown = dot(piece, spread, ((0,), (0,)))
            for h in range(2):
                value = jnp.where(even, grown[h * half : (h + 1) * half], grown[(2 + h) * half : (3 + h) * half])
                start = (j * planes + i) * half
                left[h, start : start + half, :] = jnp.where(keep, value, 0.0).astype(bf16)

    copies = []
    for step in range(degrees // SPAN):
        at = pl.ds(step * SPAN, SPAN)
        far = pl.ds(pl.multiple_of(sub * degrees + step * SPAN, 128), SPAN)
        for h in range(2):
            here = slice(h * some, (h + 1) * some)
            a = own[here, :, at].reshape(width // 2, SPAN)
            b = other[here, :, far].reshape(width // 2, SPAN)
            value = dot(left[h], jnp.concatenate([a, b], 0))
            value = value[: planes * half] + value[planes * half :]
            for i in range(planes):
                for m in range(some):
                    start = i * half + m * 2
                    result[i, h * some + m, :, at] = value[start : start + 2, :]
        copies.append(pltpu.make_async_copy(result.at[:, :, :, at], out.at[:, :, :, at], sems.at[step]))
        copies[-1].start()
    for copy in copies:
        copy.wait()


def deposit_call(part_cycle, part_pixel, part_mass, place, shell, block, basis, sky, blocks, own_degrees):
    tiles, count = part_cycle.shape[1:]
    orders, cycles, _ = basis.shape
    lanes = CYCLE_DEV * orders * 2
    bins = SHELL_DEV * blocks
    modes_tab, phase_tab = (jnp.asarray(t) for t in tables())
    anywhere = pl.BlockSpec(memory_space=pltpu.HBM)
    vmem = pl.BlockSpec(memory_space=pltpu.VMEM)
    return pl.pallas_call(
        functools.partial(deposit_kernel, blocks=blocks),
        out_shape=(
            jax.ShapeDtypeStruct((sky, bins, lanes), f32),
            jax.ShapeDtypeStruct((orders, cycles, own_degrees), bf16),
        ),
        in_specs=[anywhere] * 9,
        out_specs=(vmem, vmem),
        scratch_shapes=[
            pltpu.VMEM((1, tiles, count), jnp.int32),
            pltpu.VMEM((1, tiles, count), jnp.int32),
            pltpu.VMEM((1, tiles, count), f32),
            pltpu.VMEM((1, tiles), jnp.int32),
            pltpu.VMEM((1, tiles), jnp.int32),
            pltpu.VMEM((1, tiles), jnp.int32),
            pltpu.VMEM(modes_tab.shape, bf16),
            pltpu.VMEM(phase_tab.shape, bf16),
            pltpu.VMEM((CYCLE_DEV * tiles // TP, 2 * M, TP), f32),
            pltpu.SemaphoreType.DMA((tiles // 64, 3)),
            pltpu.SemaphoreType.DMA((6,)),
        ],
        compiler_params=pltpu.CompilerParams(vmem_limit_bytes=LIMIT),
        name="deposit",
    )(
        *(
            pltpu.with_memory_space_constraint(x, pltpu.HBM)
            for x in (
                part_cycle,
                part_pixel,
                part_mass,
                place,
                shell,
                block,
                modes_tab,
                phase_tab,
                basis,
            )
        )
    )


def legendre_call(lens_weight, own, other, parts, planes, blocks):
    orders, cycles, degrees = own.shape
    vmem = pl.BlockSpec(memory_space=pltpu.VMEM)
    return pl.pallas_call(
        functools.partial(legendre_kernel, blocks=blocks),
        out_shape=jax.ShapeDtypeStruct((planes, orders, 2, degrees), f32),
        in_specs=[pl.BlockSpec(memory_space=pltpu.SMEM), vmem, vmem] + [vmem] * len(parts),
        out_specs=pl.BlockSpec(memory_space=pltpu.HBM),
        scratch_shapes=[
            pltpu.VMEM((2, 2 * planes * orders, orders * cycles), bf16),
            pltpu.VMEM((planes, orders, 2, degrees), f32),
            pltpu.SemaphoreType.DMA((degrees // SPAN,)),
        ],
        compiler_params=pltpu.CompilerParams(vmem_limit_bytes=LIMIT),
        name="legendre",
    )(lens_weight, own, other, *parts)


def body(part_cycle, part_pixel, part_mass, tile_block, tile_shell, tile_pixel, basis, lens_weight):
    sky, sub, shells = lax.axis_size("sky"), lax.axis_size("sub"), lax.axis_size("shell")
    tiles = part_cycle.shape[1]
    _, cycles, degrees = basis.shape
    blocks = cycles * sub // CYCLE_DEV
    other = swap(basis, {})
    send, own = deposit_call(
        part_cycle,
        part_pixel,
        part_mass,
        tile_pixel,
        tile_shell,
        tile_block.reshape(1, tiles),
        basis,
        sky,
        blocks,
        degrees // sub,
    )
    parts = exchange(send)
    return legendre_call(lens_weight, own, other, parts, lens_weight.shape[0] // shells, blocks)


def solution(mesh):
    return jax.shard_map(
        body,
        mesh=mesh,
        in_specs=(
            P("shell", ("sky", "sub"), None),
            P("shell", ("sky", "sub"), None),
            P("shell", ("sky", "sub"), None),
            P("shell", ("sky", "sub"), None),
            P("shell", ("sky", "sub")),
            P("shell", ("sky", "sub")),
            P("sky", "sub", None),
            P(),
        ),
        out_specs=P(("groups", "shell"), "sky", None, "sub"),
        check_vma=False,
    )
```
